32 devices in a mesh: orb: 8 (over z, core), aux: 4 (over y, x).
Axes of the slice: x: 2, y: 2, z: 4, core: 2. Of those that a mesh axis runs over, the one named last changes fastest.
Arguments:
- three_center: bfloat16 [128, 128, 128, 128], P(('orb', 'aux')), may hold values from -0.5 to 0.5
- screening: int32 [128, 3], P(('orb', 'aux')), may hold values from -1 to 255, as said below
- density_factor: bfloat16 [32768, 128], P('orb'), may hold values from -0.23925781 to 0.23925781
- metric_inverse: bfloat16 [512, 512], replicated, may hold values from -1 to 1, as said below
Outputs:
- exchange_block: bfloat16 [1024, 256], P('orb')
The draws below stay inside these ranges and needn't reach their ends.
Inputs may be any that keep to these rules, and one draw needn't show every extreme that they name: `screening`: A device's slots are 4 consecutive rows, devices in order of orb index then aux index. Column 0 equals the orb index and column 2 the aux index of the device holding the row. Column 1 is an orbital block, or -1 for an empty slot; empty slots follow the live ones, the live orbital blocks of a device are distinct, every device has 1 to 4 live slots, and some device has 4. `metric_inverse`: Symmetric.
All inputs are finite; a program needn't handle non-finite values.
Results may differ from the reference program's by a relative error of at most 0.0063.
Values may be sent and summed in bfloat16 or wider, within the bound.
No kernel may reach another device: no remote copies, remote signals or barrier semaphores. Data moves between devices by JAX's collectives and lax.ppermute only.
A program may use at most 128 MiB of HBM per device.

```python
import jax
import jax.numpy as jnp
from jax import lax

BLOCK = 128
OCC = 128
NT_DEV = 4
NL = 256
NAUX = 512
NT = 128
N_ORB = 8
N_AUX = 4


def draw_screening(key, part):
    device_count = N_ORB * N_AUX
    sub_keys = jax.random.split(key, device_count + 3)

    def one_order(sub_key):
        return jax.random.permutation(sub_key, NL)[:NT_DEV].astype(jnp.int32)
    orders = jax.vmap(one_order)(sub_keys[:device_count])
    light_count = jax.random.randint(sub_keys[device_count], (device_count,), 1, 3)
    heavy_device = jax.random.randint(sub_keys[device_count + 1], (device_count,), 0, 8) == 0
    forced = jax.random.randint(sub_keys[device_count + 2], (), 0, device_count)
    positions = jnp.arange(device_count, dtype=jnp.int32)
    live_count = jnp.where(heavy_device | (positions == forced), NT_DEV, jnp.minimum(light_count, NT_DEV))
    slot_ids = jnp.arange(NT_DEV, dtype=jnp.int32)
    orbital = jnp.where(slot_ids[None, :] < live_count[:, None], orders, -1)
    window = jnp.broadcast_to((positions // N_AUX)[:, None], orbital.shape)
    auxiliary = jnp.broadcast_to((positions % N_AUX)[:, None], orbital.shape)
    stacked = jnp.stack([window, orbital, auxiliary], axis=-1)
    return stacked.reshape(device_count * NT_DEV, 3).astype(jnp.int32)


def draw_metric_inverse(key, part):
    sampled = jax.random.truncated_normal(key, -4.0, 4.0, (NAUX, NAUX), jnp.float32)
    symmetric = (sampled + sampled.T) * (1.0 / (2.0 * NAUX) ** 0.5)
    return symmetric.astype(jnp.bfloat16)


def block_scale(own_key, extent, cuts, least, high):
    gain = 1.0
    for position, shards_of in cuts:
        steps = jax.random.uniform(jax.random.fold_in(jax.random.fold_in(own_key, 6), position), (shards_of,), jnp.float32, least / len(cuts), high / len(cuts))
        gain = gain * jnp.repeat(jnp.exp(steps), extent[position] // shards_of).reshape((-1,) + (1,) * (len(extent) - 1 - position))
    return gain


def centred(stream_key, shape, spread, limit, cuts=(), held_as=jnp.bfloat16):
    result = jax.random.normal(stream_key, shape, jnp.float32) * spread
    if len(cuts) > 0:
        result = block_scale(stream_key, shape, cuts, -0.22, 0.18) * result
    return jnp.clip(result, min=-limit, max=limit).astype(held_as)


def setup_inputs(seed: int = 0) -> dict:
    arg_keys = jax.random.split(jax.random.key(seed), 5)
    three_center = centred(arg_keys[0], (NT, BLOCK, BLOCK, BLOCK), BLOCK ** -0.5, 0.5, ((0, 32),))
    screening = draw_screening(jax.random.fold_in(arg_keys[4], 71), 0)
    density_factor = centred(arg_keys[2], (NL * BLOCK, OCC), 0.04, 0.23925781, ((0, 8),))
    metric_inverse = draw_metric_inverse(jax.random.fold_in(arg_keys[4], 71), 0)
    return {"three_center": three_center, "screening": screening, "density_factor": density_factor, "metric_inverse": metric_inverse}


def keep_same(current):
    return current


def reference(three_center, screening, density_factor, metric_inverse):
    slot_total = three_center.shape[0]
    factor_blocks = density_factor.reshape(NL, BLOCK, OCC)

    def pair_half(group):
        window_id = group // N_AUX
        aux_id = group % N_AUX

        def one_slot(slot_index, carried):
            orbital = screening[slot_index, 1]
            hit = (screening[slot_index, 0] == window_id) & (screening[slot_index, 2] == aux_id) & (orbital >= 0)

            def add_tile(current):
                row_block = lax.dynamic_index_in_dim(factor_blocks, jnp.maximum(orbital, 0), 0, keepdims=False)
                tile_now = lax.dynamic_index_in_dim(three_center, slot_index, 0, keepdims=False)
                return current + jnp.einsum("mlp,li->mip", tile_now.astype(jnp.float32), row_block.astype(jnp.float32))

            return lax.cond(hit, add_tile, keep_same, carried)

        zero_start = jnp.zeros((BLOCK, OCC, BLOCK), jnp.float32)
        summed = lax.fori_loop(0, slot_total, one_slot, zero_start)
        return summed.astype(jnp.bfloat16)

    halves = lax.map(pair_half, jnp.arange(N_ORB * N_AUX, dtype=jnp.int32))
    halves = halves.reshape(N_ORB, N_AUX, BLOCK, OCC, BLOCK).transpose(0, 2, 3, 1, 4).reshape(N_ORB, BLOCK, OCC, NAUX)
    metric_full = metric_inverse.astype(jnp.float32)

    def window_row(window_id):
        own_half = halves[window_id].astype(jnp.float32)
        next_half = halves[(window_id + 1) % N_ORB].astype(jnp.float32)
        fitted = jnp.einsum("miP,PQ->miQ", own_half, metric_full).astype(jnp.bfloat16)
        fitted = lax.optimization_barrier(fitted).astype(jnp.float32)
        diagonal = jnp.einsum("miq,niq->mn", fitted, own_half)
        coupling = jnp.einsum("miq,niq->mn", fitted, next_half)
        return jnp.concatenate([diagonal, coupling], axis=1).astype(jnp.bfloat16)

    blocks_out = lax.map(window_row, jnp.arange(N_ORB, dtype=jnp.int32))
    return blocks_out.reshape(N_ORB * BLOCK, 2 * BLOCK)
```

```python
import functools

import jax
import jax.numpy as jnp
from jax import lax
from jax.experimental import pallas as pl
from jax.experimental.pallas import tpu as pltpu
from jax.sharding import PartitionSpec as P


CHUNKS = 2
STEP_ROWS = 16


def pick_kernel(owned, block, slot_count, *refs):
    place_ref, own_ref, partner_ref = refs[:3]
    wanted = refs[3 : 3 + (len(refs) - 3) // 2]
    given = refs[3 + (len(refs) - 3) // 2 :]
    base, core = place_ref[0], place_ref[1]
    for want_ref, give_ref in zip(wanted, given):
        for slot in range(slot_count):
            orbital = want_ref[slot]
            local = orbital - base
            inside = (orbital >= 0) & (local >= 0) & (local < 2 * owned)
            upper = local >= owned
            row = pl.multiple_of(
                jnp.clip(jnp.where(upper, local - owned, local), 0, owned - 1) * block, block
            )
            mine = inside & (upper == (core == 1))

            @pl.when(mine)
            def _():
                give_ref[slot] = own_ref[pl.ds(row, block), :]

            @pl.when(inside & jnp.logical_not(mine))
            def _():
                give_ref[slot] = partner_ref[pl.ds(row, block), :]

            @pl.when(jnp.logical_not(inside))
            def _():
                give_ref[slot] = jnp.zeros_like(give_ref[slot])


def half_kernel(aux_count, chunk_rows, *refs):
    part_count = len(refs) - 4 - aux_count * len(chunk_rows)
    place_ref, tile_ref = refs[0], refs[1]
    parts = refs[2 : 2 + part_count - 1]
    outs = refs[1 + part_count : -3]
    plain, ordered, wide = refs[-3:]
    slot_count, rows, block, _ = tile_ref.shape
    occupied = ordered.shape[0]
    share = occupied // aux_count

    @pl.when(pl.program_id(0) == 0)
    def _():
        for slot in range(slot_count):
            total = parts[0][slot].astype(jnp.float32)
            for part in parts[1:]:
                total = total + part[slot].astype(jnp.float32)
            plain[:, slot * block : (slot + 1) * block] = total.T
        for away in range(aux_count):
            start = pl.multiple_of((place_ref[2] ^ away) * share, share)
            ordered[away * share : (away + 1) * share, :] = plain[pl.ds(start, share), :].astype(
                jnp.bfloat16
            )

    left = ordered[...]
    for row in range(0, rows, 2):
        right = jnp.concatenate(
            [
                tile_ref[:, row].reshape(slot_count * block, block),
                tile_ref[:, row + 1].reshape(slot_count * block, block),
            ],
            axis=1,
        )
        product = jnp.dot(left, right, preferred_element_type=jnp.float32)
        wide[pl.ds(row, occupied, stride=rows), :] = product[:, :block]
        wide[pl.ds(row + 1, occupied, stride=rows), :] = product[:, block:]
    index = 0
    for away in range(aux_count):
        first = away * share
        for count in chunk_rows:
            outs[index][...] = (
                wide[first * rows : (first + count) * rows, :]
                .reshape(count, rows, block)
                .astype(jnp.bfloat16)
            )
            first += count
            index += 1


def fit_kernel(aux_count, *refs):
    place_ref, metric_ref = refs[:2]
    parts = refs[2 : 2 + aux_count]
    before_ref, fitted_ref, after_ref, turned = refs[2 + aux_count :]
    count, block, width = parts[0].shape
    me = place_ref[2]
    for row in range(aux_count):
        for column in range(aux_count):
            turned[row * width : (row + 1) * width, column * width : (column + 1) * width] = metric_ref[
                pl.ds(pl.multiple_of((me ^ row) * width, width), width),
                pl.ds(pl.multiple_of((me ^ column) * width, width), width),
            ]
    metric = turned[...]
    total = before_ref[...]
    for i in range(count):
        half = jnp.concatenate([part[i] for part in parts], axis=1)
        fitted = jnp.dot(half, metric, preferred_element_type=jnp.float32).astype(jnp.bfloat16)
        fitted_ref[i] = fitted
        total = total + lax.dot_general(
            fitted, half, (((1,), (1,)), ((), ())), preferred_element_type=jnp.float32
        )
    after_ref[...] = total


def couple_kernel(aux_count, *refs):
    fitted_ref = refs[0]
    parts = refs[1 : 1 + aux_count]
    before_ref, after_ref = refs[1 + aux_count :]
    total = before_ref[...]
    for i in range(fitted_ref.shape[0]):
        half = jnp.concatenate([part[i] for part in parts], axis=1)
        total = total + lax.dot_general(
            fitted_ref[i], half, (((1,), (1,)), ((), ())), preferred_element_type=jnp.float32
        )
    after_ref[...] = total


def on_device(orb_count, aux_count, three_center, screening, density_factor, metric_inverse):
    slot_count, block = three_center.shape[:2]
    occupied = density_factor.shape[1]
    owned = density_factor.shape[0] // block
    share = occupied // aux_count
    chunks = CHUNKS
    chunk_rows = (share // chunks,) * chunks
    smem = pl.BlockSpec(memory_space=pltpu.SMEM)
    vmem = pl.BlockSpec(memory_space=pltpu.VMEM)
    bf16, f32 = jnp.bfloat16, jnp.float32

    orb = lax.axis_index("orb")
    aux = lax.axis_index("aux")
    place = jnp.stack([orb // 2 * (2 * owned), orb % 2, aux]).astype(jnp.int32)

    def along_orb(x, by):
        return lax.ppermute(x, "orb", [(i, (i + by) % orb_count) for i in range(orb_count)])

    def across_aux(x, away):
        return lax.ppermute(x, "aux", [(i, i ^ away) for i in range(aux_count)])

    orbitals = screening[:, 1]
    partner = lax.ppermute(density_factor, "orb", [(i, i ^ 1) for i in range(orb_count)])
    shifts = list(range(2, orb_count, 2))
    wanted = [orbitals] + [along_orb(orbitals, by) for by in shifts]
    given = pl.pallas_call(
        functools.partial(pick_kernel, owned, block, slot_count),
        out_shape=[jax.ShapeDtypeStruct((slot_count, block, occupied), bf16)] * len(wanted),
        in_specs=[smem, vmem, vmem] + [smem] * len(wanted),
        out_specs=[vmem] * len(wanted),
        cost_estimate=pl.CostEstimate(flops=0, bytes_accessed=4 << 20, transcendentals=0),
        name="pick",
    )(place, density_factor, partner, *wanted)
    arrived = [given[0]] + [along_orb(x, -by) for x, by in zip(given[1:], shifts)]

    rows = STEP_ROWS
    whole = pl.BlockSpec((slot_count, block, occupied), lambda j: (0, 0, 0))
    halves = pl.pallas_call(
        functools.partial(half_kernel, aux_count, chunk_rows),
        grid=(block // rows,),
        out_shape=[
            jax.ShapeDtypeStruct((count, block, block), bf16)
            for _ in range(aux_count)
            for count in chunk_rows
        ],
        in_specs=[smem, pl.BlockSpec((slot_count, rows, block, block), lambda j: (0, j, 0, 0))]
        + [whole] * len(arrived),
        out_specs=[
            pl.BlockSpec((count, rows, block), lambda j: (0, j, 0))
            for _ in range(aux_count)
            for count in chunk_rows
        ],
        scratch_shapes=[
            pltpu.VMEM((occupied, slot_count * block), f32),
            pltpu.VMEM((occupied, slot_count * block), bf16),
            pltpu.VMEM((occupied * rows, block), f32),
        ],
        cost_estimate=pl.CostEstimate(
            flops=2 * slot_count * block**3 * occupied, bytes_accessed=20 << 20, transcendentals=0
        ),
        name="half",
    )(place, three_center, *arrived)
    halves = [halves[away * chunks : (away + 1) * chunks] for away in range(aux_count)]

    diagonal = jnp.zeros((block, block), f32)
    coupling = jnp.zeros((block, block), f32)
    here = [
        [halves[0][c]] + [across_aux(halves[away][c], away) for away in range(1, aux_count)]
        for c in range(chunks)
    ]
    following = [[along_orb(x, -1) for x in here[c]] for c in range(chunks)]
    for c in range(chunks):
        count = chunk_rows[c]
        width = aux_count * block
        fitted, diagonal = pl.pallas_call(
            functools.partial(fit_kernel, aux_count),
            out_shape=[
                jax.ShapeDtypeStruct((count, block, width), bf16),
                jax.ShapeDtypeStruct((block, block), f32),
            ],
            in_specs=[smem] + [vmem] * (aux_count + 2),
            out_specs=[vmem] * 2,
            scratch_shapes=[pltpu.VMEM((width, width), bf16)],
            cost_estimate=pl.CostEstimate(
                flops=2 * count * block * width * (width + block), bytes_accessed=4 << 20, transcendentals=0
            ),
            name="fit",
        )(place, metric_inverse, *here[c], diagonal)
        coupling = pl.pallas_call(
            functools.partial(couple_kernel, aux_count),
            out_shape=jax.ShapeDtypeStruct((block, block), f32),
            in_specs=[vmem] * (aux_count + 2),
            out_specs=vmem,
            cost_estimate=pl.CostEstimate(
                flops=2 * count * block * width * block, bytes_accessed=4 << 20, transcendentals=0
            ),
            name="couple",
        )(fitted, *following[c], coupling)

    def sum_aux(x):
        terms = [x] + [across_aux(x, away) for away in range(1, aux_count)]
        while len(terms) > 1:
            terms = [a + b for a, b in zip(terms[::2], terms[1::2])]
        return terms[0].astype(bf16)

    return jnp.concatenate([sum_aux(diagonal), sum_aux(coupling)], axis=1)


def solution(mesh):
    placed = (P(("orb", "aux"), None, None, None), P(("orb", "aux"), None), P("orb", None), P())
    body = functools.partial(on_device, mesh.shape["orb"], mesh.shape["aux"])
    return jax.shard_map(
        body, mesh=mesh, in_specs=placed, out_specs=P("orb", None), check_vma=False
    )
```

```python
import functools

import jax
import jax.numpy as jnp
from jax import lax
from jax.experimental import pallas as pl
from jax.experimental.pallas import tpu as pltpu
from jax.sharding import PartitionSpec as P


PARTS = (1, 1)
STEP_ROWS = 16
GROUP = 4
VMEM = pltpu.VMEM
SMEM_SPEC = pl.BlockSpec(memory_space=pltpu.SMEM)
VMEM_SPEC = pl.BlockSpec(memory_space=pltpu.VMEM)


def local_call(kernel, out_shape, operands, scalars, flops, scratch=()):
    operands = [pltpu.with_memory_space_constraint(x, VMEM) for x in operands]
    out_shape = jax.tree.map(lambda x: VMEM(x.shape, x.dtype), out_shape)
    return pl.pallas_call(
        kernel,
        out_shape=out_shape,
        in_specs=[SMEM_SPEC] * len(scalars) + [VMEM_SPEC] * len(operands),
        out_specs=jax.tree.map(lambda _: VMEM_SPEC, out_shape),
        scratch_shapes=list(scratch),
        cost_estimate=pl.CostEstimate(flops=flops, bytes_accessed=1 << 20, transcendentals=0),
        compiler_params=pltpu.CompilerParams(vmem_limit_bytes=12 << 20),
    )(*scalars, *operands)


def load_kernel(first, source_ref, loaded_ref, sems):
    copies = [
        pltpu.make_async_copy(source_ref.at[first + slot], loaded_ref.at[slot], sems.at[slot])
        for slot in range(loaded_ref.shape[0])
    ]
    for copy in copies:
        copy.start()
    for copy in copies:
        copy.wait()


def load(source, first, count):
    return pl.pallas_call(
        functools.partial(load_kernel, first),
        out_shape=VMEM((count, *source.shape[1:]), source.dtype),
        in_specs=[pl.BlockSpec(memory_space=pl.ANY)],
        out_specs=VMEM_SPEC,
        scratch_shapes=[pltpu.SemaphoreType.DMA((count,))],
        cost_estimate=pl.CostEstimate(
            flops=0, bytes_accessed=count * source[0].size * source.dtype.itemsize, transcendentals=0
        ),
        compiler_params=pltpu.CompilerParams(vmem_limit_bytes=1 << 20),
        name="load",
    )(source)


def pick_kernel(owned, block, slot_count, aux_count, chunk_rows, *refs):
    dest_count = (len(refs) - 4) // (1 + len(chunk_rows))
    place_ref = refs[0]
    wanted = refs[1 : 1 + dest_count]
    own_ref, partner_ref = refs[1 + dest_count : 3 + dest_count]
    given = refs[3 + dest_count : -1]
    turned = refs[-1]
    base, core, me = place_ref[0], place_ref[1], place_ref[2]
    share = turned.shape[0] // aux_count
    for dest in range(dest_count):
        for slot in range(slot_count):
            orbital = wanted[dest][slot, 1]
            local = orbital - base
            inside = (orbital >= 0) & (local >= 0) & (local < 2 * owned)
            upper = jnp.where(local >= owned, 1, 0)
            row = jnp.clip(local - upper * owned, 0, owned - 1) * block
            rows = pl.ds(pl.multiple_of(row, block), block)
            picked = jnp.where(
                upper == core, own_ref[rows, :].astype(jnp.float32), partner_ref[rows, :].astype(jnp.float32)
            )
            picked = jnp.where(inside, picked, jnp.zeros_like(picked))
            turned[...] = picked.T
            for away in range(aux_count):
                start = pl.multiple_of((me ^ away) * share, share)
                first = 0
                for chunk, count in enumerate(chunk_rows):
                    given[dest * len(chunk_rows) + chunk][slot, away * count : (away + 1) * count, :] = turned[
                        pl.ds(start + first, count), :
                    ].astype(jnp.bfloat16)
                    first += count


def half_kernel(aux_count, tile_count, *refs):
    tiles = refs[:tile_count]
    parts = refs[tile_count : -1 - aux_count]
    outs = refs[-1 - aux_count : -1]
    wide = refs[-1]
    slot_count, block = parts[0].shape[0], tiles[0].shape[1]
    width = parts[0].shape[1]
    count = width // aux_count
    rows = STEP_ROWS
    stride = rows + 1
    columns = []
    for slot in range(slot_count):
        total = parts[0][slot].astype(jnp.float32)
        for part in parts[1:]:
            total = total + part[slot].astype(jnp.float32)
        columns.append(total.astype(jnp.bfloat16))
    left = jnp.concatenate(columns, axis=1)

    def step(index, carry):
        base = pl.multiple_of(index * rows, rows)
        for row in range(0, rows, 2):
            right = jnp.concatenate(
                [
                    jnp.concatenate(
                        [tile[:, base + row + m].reshape(-1, block) for tile in tiles], axis=0
                    )
                    for m in range(2)
                ],
                axis=1,
            )
            product = jnp.dot(left, right, preferred_element_type=jnp.float32)
            wide[pl.ds(row, width, stride=stride), :] = product[:, :block]
            wide[pl.ds(row + 1, width, stride=stride), :] = product[:, block:]
        for away in range(aux_count):
            for i in range(count):
                outs[away][i, pl.ds(base, rows), :] = wide[
                    pl.ds((away * count + i) * stride, rows), :
                ].astype(jnp.bfloat16)
        return carry

    lax.fori_loop(0, block // rows, step, 0)


def gram(left_ref, right_parts):
    count = left_ref.shape[0]
    left = jnp.concatenate([left_ref[i] for i in range(count)], axis=1)
    right = jnp.concatenate([part[i] for i in range(count) for part in right_parts], axis=1)
    return lax.dot_general(left, right, (((1,), (1,)), ((), ())), preferred_element_type=jnp.float32)


def fit_kernel(aux_count, *refs):
    place_ref, metric_ref = refs[:2]
    parts = refs[2 : 2 + aux_count]
    before = refs[2 + aux_count : -3]
    fitted_ref, after_ref, turned = refs[-3:]
    count, block, width = parts[0].shape
    me = place_ref[2]
    for row in range(aux_count):
        for column in range(aux_count):
            turned[row * width : (row + 1) * width, column * width : (column + 1) * width] = metric_ref[
                pl.ds(pl.multiple_of((me ^ row) * width, width), width),
                pl.ds(pl.multiple_of((me ^ column) * width, width), width),
            ]
    metric = turned[...]
    for first in range(0, count, GROUP):
        here = min(GROUP, count - first)
        half = jnp.concatenate(
            [part[first : first + here].reshape(here * block, width) for part in parts], axis=1
        )
        fitted = jnp.dot(half, metric, preferred_element_type=jnp.float32).astype(jnp.bfloat16)
        fitted_ref[first : first + here] = fitted.reshape(here, block, aux_count * width)
    total = gram(fitted_ref, parts)
    for ref in before:
        total = total + ref[...]
    after_ref[...] = total


def couple_kernel(aux_count, *refs):
    total = gram(refs[0], refs[1 : 1 + aux_count])
    for ref in refs[1 + aux_count : -1]:
        total = total + ref[...]
    refs[-1][...] = total


def on_device(orb_count, aux_count, three_center, screening, density_factor, metric_inverse):
    slot_count, block = three_center.shape[:2]
    occupied = density_factor.shape[1]
    owned = density_factor.shape[0] // block
    share = occupied // aux_count
    chunk_rows = [share * part // sum(PARTS) for part in PARTS]
    chunks = len(chunk_rows)
    bf16, f32 = jnp.bfloat16, jnp.float32

    orb = lax.axis_index("orb")
    aux = lax.axis_index("aux")
    place = jnp.stack([(orb >> 1) * (2 * owned), orb & 1, aux]).astype(jnp.int32)

    def along_orb(x, by):
        return lax.ppermute(x, "orb", [(i, (i + by) % orb_count) for i in range(orb_count)])

    def across_aux(x, away):
        return lax.ppermute(x, "aux", [(i, i ^ away) for i in range(aux_count)])

    loads = []
    for number in range(2):
        loads.append(load(three_center, number * (slot_count // 2), slot_count // 2))
    partner = lax.ppermute(density_factor, "orb", [(i, i ^ 1) for i in range(orb_count)])
    shifts = list(range(2, orb_count, 2))
    wanted = [screening]
    for by in shifts:
        wanted.append(along_orb(screening, by))
    given = local_call(
        functools.partial(pick_kernel, owned, block, slot_count, aux_count, chunk_rows),
        [jax.ShapeDtypeStruct((slot_count, aux_count * count, block), bf16) for _ in wanted for count in chunk_rows],
        [density_factor, partner],
        [place, *wanted],
        0,
        [pltpu.VMEM((occupied, block), f32)],
    )
    here, following = [], []
    for c, count in enumerate(chunk_rows):
        arrived = [given[c]]
        for dest, by in enumerate(shifts, 1):
            arrived.append(along_orb(given[dest * chunks + c], -by))
        halves = local_call(
            functools.partial(half_kernel, aux_count, len(loads)),
            [jax.ShapeDtypeStruct((count, block, block), bf16)] * aux_count,
            [*loads, *arrived],
            [],
            2 * slot_count * block**3 * count * aux_count,
            [pltpu.VMEM((aux_count * count * (STEP_ROWS + 1), block), f32)],
        )
        mine, theirs = [halves[0]], []
        for away in range(1, aux_count):
            mine.append(across_aux(halves[away], away))
        for away in range(aux_count):
            theirs.append(along_orb(mine[away], -1))
        here.append(mine)
        following.append(theirs)

    diagonal, coupling = [], []
    width = aux_count * block
    for c, count in enumerate(chunk_rows):
        fitted, *diagonal = local_call(
            functools.partial(fit_kernel, aux_count),
            [
                jax.ShapeDtypeStruct((count, block, width), bf16),
                jax.ShapeDtypeStruct((block, block), f32),
            ],
            [metric_inverse, *here[c], *diagonal],
            [place],
            2 * count * block * width * (width + block),
            [pltpu.VMEM((width, width), bf16)],
        )
        coupling = [
            local_call(
                functools.partial(couple_kernel, aux_count),
                jax.ShapeDtypeStruct((block, block), f32),
                [fitted, *following[c], *coupling],
                [],
                2 * count * block * width * block,
            )
        ]

    def sum_aux(x):
        terms = {}
        for away in reversed(range(1, aux_count)):
            terms[away] = across_aux(x, away)
        terms = [x] + [terms[away] for away in range(1, aux_count)]
        while len(terms) > 1:
            terms = [a + b for a, b in zip(terms[::2], terms[1::2])]
        return terms[0].astype(bf16)

    return jnp.concatenate([sum_aux(diagonal[0]), sum_aux(coupling[0])], axis=1)


def solution(mesh):
    placed = (P(("orb", "aux"), None, None, None), P(("orb", "aux"), None), P("orb", None), P())
    sizes = mesh.shape["orb"], mesh.shape["aux"]

    def body(*args):
        return on_device(*sizes, *args)

    return jax.shard_map(body, mesh=mesh, in_specs=placed, out_specs=P("orb", None), check_vma=False)
```

```python
import functools

import jax
import jax.numpy as jnp
from jax import lax
from jax.experimental import pallas as pl
from jax.experimental.pallas import tpu as pltpu
from jax.sharding import PartitionSpec as P


PARTS = (1, 1)
PIECES = (2, 2)
STEP_ROWS = 16
GROUP = 4
LONG = 20_000_000_000
VMEM = pltpu.VMEM
SMEM_SPEC = pl.BlockSpec(memory_space=pltpu.SMEM)
VMEM_SPEC = pl.BlockSpec(memory_space=pltpu.VMEM)


def local_call(kernel, out_shape, operands, scalars, flops, scratch=()):
    operands = [pltpu.with_memory_space_constraint(x, VMEM) for x in operands]
    out_shape = jax.tree.map(lambda x: VMEM(x.shape, x.dtype), out_shape)
    return pl.pallas_call(
        kernel,
        out_shape=out_shape,
        in_specs=[SMEM_SPEC] * len(scalars) + [VMEM_SPEC] * len(operands),
        out_specs=jax.tree.map(lambda _: VMEM_SPEC, out_shape),
        scratch_shapes=list(scratch),
        cost_estimate=pl.CostEstimate(flops=flops, bytes_accessed=1 << 20, transcendentals=0),
        compiler_params=pltpu.CompilerParams(vmem_limit_bytes=12 << 20),
    )(*scalars, *operands)


def turn_kernel(aux_count, place_ref, metric_ref, turned_ref):
    width = metric_ref.shape[0] // aux_count
    me = place_ref[2]
    for row in range(aux_count):
        for column in range(aux_count):
            turned_ref[row * width : (row + 1) * width, column * width : (column + 1) * width] = (
                metric_ref[
                    pl.ds(pl.multiple_of((me ^ row) * width, width), width),
                    pl.ds(pl.multiple_of((me ^ column) * width, width), width),
                ]
            )


def pick_kernel(owned, block, slot_count, aux_count, chunk_rows, *refs):
    dest_count = (len(refs) - 4) // (1 + len(chunk_rows))
    place_ref = refs[0]
    wanted = refs[1 : 1 + dest_count]
    own_ref, partner_ref = refs[1 + dest_count : 3 + dest_count]
    given = refs[3 + dest_count : -1]
    turned = refs[-1]
    base, core, me = place_ref[0], place_ref[1], place_ref[2]
    share = turned.shape[0] // aux_count
    for dest in range(dest_count):
        for slot in range(slot_count):
            orbital = wanted[dest][slot, 1]
            local = orbital - base
            inside = (orbital >= 0) & (local >= 0) & (local < 2 * owned)
            upper = jnp.where(local >= owned, 1, 0)
            row = jnp.clip(local - upper * owned, 0, owned - 1) * block
            rows = pl.ds(pl.multiple_of(row, block), block)
            picked = jnp.where(
                upper == core, own_ref[rows, :].astype(jnp.float32), partner_ref[rows, :].astype(jnp.float32)
            )
            picked = jnp.where(inside, picked, jnp.zeros_like(picked))
            turned[...] = picked.T
            for away in range(aux_count):
                start = pl.multiple_of((me ^ away) * share, share)
                first = 0
                for chunk, count in enumerate(chunk_rows):
                    given[dest * len(chunk_rows) + chunk][slot, away * count : (away + 1) * count, :] = turned[
                        pl.ds(start + first, count), :
                    ].astype(jnp.bfloat16)
                    first += count


def half_kernel(out_count, *refs):
    tile_ref = refs[0]
    parts = refs[1 : -1 - out_count]
    outs = refs[-1 - out_count : -1]
    wide = refs[-1]
    slot_count, block = tile_ref.shape[:2]
    width = parts[0].shape[1]
    rows = STEP_ROWS
    stride = rows + 1
    columns = []
    for slot in range(slot_count):
        total = parts[0][slot].astype(jnp.float32)
        for part in parts[1:]:
            total = total + part[slot].astype(jnp.float32)
        columns.append(total.astype(jnp.bfloat16))
    left = jnp.concatenate(columns, axis=1)

    def step(index, carry):
        base = pl.multiple_of(index * rows, rows)
        for row in range(0, rows, 2):
            right = jnp.concatenate(
                [
                    tile_ref[:, base + row + m].reshape(slot_count * block, block) for m in range(2)
                ],
                axis=1,
            )
            product = jnp.dot(left, right, preferred_element_type=jnp.float32)
            wide[pl.ds(row, width, stride=stride), :] = product[:, :block]
            wide[pl.ds(row + 1, width, stride=stride), :] = product[:, block:]
        first = 0
        for out in outs:
            for i in range(out.shape[0]):
                out[i, pl.ds(base, rows), :] = wide[pl.ds((first + i) * stride, rows), :].astype(
                    jnp.bfloat16
                )
            first += out.shape[0]
        return carry

    lax.fori_loop(0, block // rows, step, 0)


def gram(fitted, parts, first):
    count = len(fitted)
    right = [
        part[i if part is parts[-1] else first + i] for i in range(count) for part in parts
    ]
    return lax.dot_general(
        jnp.concatenate(fitted, axis=1),
        jnp.concatenate(right, axis=1),
        (((1,), (1,)), ((), ())),
        preferred_element_type=jnp.float32,
    )


def fit_kernel(aux_count, first, *refs):
    metric_ref = refs[0]
    parts = refs[1 : 1 + aux_count]
    before = refs[1 + aux_count : -2]
    fitted_ref, after_ref = refs[-2:]
    count, block, width = parts[-1].shape
    metric = metric_ref[...]
    for start in range(0, count, GROUP):
        here = min(GROUP, count - start)
        rows = [part[first + start : first + start + here] for part in parts[:-1]]
        rows.append(parts[-1][start : start + here])
        half = jnp.concatenate([x.reshape(here * block, width) for x in rows], axis=1)
        fitted = jnp.dot(half, metric, preferred_element_type=jnp.float32).astype(jnp.bfloat16)
        fitted_ref[start : start + here] = fitted.reshape(here, block, aux_count * width)
    total = gram([fitted_ref[i] for i in range(count)], parts, first)
    for ref in before:
        total = total + ref[...]
    after_ref[...] = total


def couple_kernel(aux_count, first, final, *refs):
    total = gram([refs[0][i] for i in range(refs[0].shape[0])], refs[1 : 1 + aux_count], first)
    before = refs[1 + aux_count : -1]
    if final:
        before, diagonal = before[:-1], before[-1]
    for ref in before:
        total = total + ref[...]
    if final:
        block = total.shape[0]
        refs[-1][:, :block] = diagonal[...].astype(jnp.bfloat16)
        refs[-1][:, block:] = total.astype(jnp.bfloat16)
    else:
        refs[-1][...] = total


def on_device(orb_count, aux_count, three_center, screening, density_factor, metric_inverse):
    slot_count, block = three_center.shape[:2]
    occupied = density_factor.shape[1]
    owned = density_factor.shape[0] // block
    share = occupied // aux_count
    chunk_rows = [share * part // sum(PARTS) for part in PARTS]
    chunks = len(chunk_rows)
    bf16, f32 = jnp.bfloat16, jnp.float32

    orb = lax.axis_index("orb")
    aux = lax.axis_index("aux")
    place = jnp.stack([(orb >> 1) * (2 * owned), orb & 1, aux]).astype(jnp.int32)

    def along_orb(x, by):
        return lax.ppermute(x, "orb", [(i, (i + by) % orb_count) for i in range(orb_count)])

    def same_core(x, chip):
        return lax.ppermute(x, "orb", [(i, i ^ (2 * chip)) for i in range(orb_count)])

    def across_aux(x, away):
        return lax.ppermute(x, "aux", [(i, i ^ away) for i in range(aux_count)])

    turned = local_call(
        functools.partial(turn_kernel, aux_count),
        jax.ShapeDtypeStruct(metric_inverse.shape, bf16),
        [metric_inverse],
        [place],
        LONG,
    )
    partner = lax.ppermute(density_factor, "orb", [(i, i ^ 1) for i in range(orb_count)])
    wanted = [screening]
    chips = range(1, orb_count // 2)
    for chip in chips:
        wanted.append(same_core(screening, chip))
    given = local_call(
        functools.partial(pick_kernel, owned, block, slot_count, aux_count, chunk_rows),
        [
            jax.ShapeDtypeStruct((slot_count, aux_count * count, block), bf16)
            for _ in wanted
            for count in chunk_rows
        ],
        [density_factor, partner],
        [place, *wanted],
        LONG,
        [pltpu.VMEM((occupied, block), f32)],
    )
    last = aux_count - 1
    pieces = []
    for c, count in enumerate(chunk_rows):
        arrived = [given[c]]
        for chip in chips:
            arrived.append(same_core(given[chip * chunks + c], chip))
        piece_rows = count // PIECES[c]
        out_rows = [count] * last + [piece_rows] * PIECES[c]
        halves = local_call(
            functools.partial(half_kernel, len(out_rows)),
            [jax.ShapeDtypeStruct((rows, block, block), bf16) for rows in out_rows],
            [three_center, *arrived],
            [],
            2 * slot_count * block**3 * count * aux_count,
            [pltpu.VMEM((aux_count * count * (STEP_ROWS + 1), block), f32)],
        )
        mine, theirs = [halves[0]], []
        for away in range(1, last):
            mine.append(across_aux(halves[away], away))
        for away in range(last):
            theirs.append(along_orb(mine[away], -1))
        for j in range(PIECES[c]):
            mine_piece = across_aux(halves[last + j], last)
            their_piece = along_orb(mine_piece, -1)
            pieces.append((c, j, piece_rows, mine + [mine_piece], theirs + [their_piece]))

    diagonal, coupling = [], []
    width = aux_count * block
    for number, (c, j, count, mine, theirs) in enumerate(pieces):
        final = number == len(pieces) - 1
        fitted, *diagonal = local_call(
            functools.partial(fit_kernel, aux_count, j * count),
            [
                jax.ShapeDtypeStruct((count, block, width), bf16),
                jax.ShapeDtypeStruct((block, block), f32),
            ],
            [turned, *mine, *diagonal],
            [],
            2 * count * block * width * (width + block),
        )
        coupling = [
            local_call(
                functools.partial(couple_kernel, aux_count, j * count, final),
                jax.ShapeDtypeStruct((block, 2 * block), bf16)
                if final
                else jax.ShapeDtypeStruct((block, block), f32),
                [fitted, *theirs, *coupling, *(diagonal if final else [])],
                [],
                2 * count * block * width * block,
            )
        ]

    terms = {0: coupling[0]}
    for away in reversed(range(1, aux_count)):
        terms[away] = across_aux(coupling[0], away)
    terms = [terms[away].astype(f32) for away in range(aux_count)]
    while len(terms) > 1:
        terms = [a + b for a, b in zip(terms[::2], terms[1::2])]
    return terms[0].astype(bf16)


def solution(mesh):
    placed = (P(("orb", "aux"), None, None, None), P(("orb", "aux"), None), P("orb", None), P())
    sizes = mesh.shape["orb"], mesh.shape["aux"]

    def body(*args):
        return on_device(*sizes, *args)

    return jax.shard_map(body, mesh=mesh, in_specs=placed, out_specs=P("orb", None), check_vma=False)
```

```python
import functools

import jax
import jax.numpy as jnp
from jax import lax
from jax.experimental import pallas as pl
from jax.experimental.pallas import tpu as pltpu
from jax.sharding import PartitionSpec as P


PARTS = (3, 5)
PIECES = ((1, 1), (3, 2))
STEP_ROWS = 16
GROUP = 4
LONG = 20_000_000_000
VMEM = pltpu.VMEM
SMEM_SPEC = pl.BlockSpec(memory_space=pltpu.SMEM)
VMEM_SPEC = pl.BlockSpec(memory_space=pltpu.VMEM)


def local_call(kernel, out_shape, operands, scalars, flops, scratch=()):
    operands = [pltpu.with_memory_space_constraint(x, VMEM) for x in operands]
    out_shape = jax.tree.map(lambda x: VMEM(x.shape, x.dtype), out_shape)
    return pl.pallas_call(
        kernel,
        out_shape=out_shape,
        in_specs=[SMEM_SPEC] * len(scalars) + [VMEM_SPEC] * len(operands),
        out_specs=jax.tree.map(lambda _: VMEM_SPEC, out_shape),
        scratch_shapes=list(scratch),
        cost_estimate=pl.CostEstimate(flops=flops, bytes_accessed=1 << 20, transcendentals=0),
        compiler_params=pltpu.CompilerParams(vmem_limit_bytes=12 << 20),
    )(*scalars, *operands)


def turn_kernel(aux_count, place_ref, metric_ref, turned_ref):
    width = metric_ref.shape[0] // aux_count
    me = place_ref[2]
    for row in range(aux_count):
        for column in range(aux_count):
            turned_ref[row * width : (row + 1) * width, column * width : (column + 1) * width] = (
                metric_ref[
                    pl.ds(pl.multiple_of((me ^ row) * width, width), width),
                    pl.ds(pl.multiple_of((me ^ column) * width, width), width),
                ]
            )


def pick_kernel(owned, block, slot_count, aux_count, chunk_rows, *refs):
    dest_count = (len(refs) - 4) // (1 + len(chunk_rows))
    place_ref = refs[0]
    wanted = refs[1 : 1 + dest_count]
    own_ref, partner_ref = refs[1 + dest_count : 3 + dest_count]
    given = refs[3 + dest_count : -1]
    turned = refs[-1]
    base, core, me = place_ref[0], place_ref[1], place_ref[2]
    share = turned.shape[0] // aux_count
    for dest in range(dest_count):
        for slot in range(slot_count):
            orbital = wanted[dest][slot, 1]
            local = orbital - base
            inside = (orbital >= 0) & (local >= 0) & (local < 2 * owned)
            upper = jnp.where(local >= owned, 1, 0)
            row = jnp.clip(local - upper * owned, 0, owned - 1) * block
            rows = pl.ds(pl.multiple_of(row, block), block)
            picked = jnp.where(
                upper == core, own_ref[rows, :].astype(jnp.float32), partner_ref[rows, :].astype(jnp.float32)
            )
            picked = jnp.where(inside, picked, jnp.zeros_like(picked))
            turned[...] = picked.T
            for away in range(aux_count):
                start = pl.multiple_of((me ^ away) * share, share)
                first = 0
                for chunk, count in enumerate(chunk_rows):
                    given[dest * len(chunk_rows) + chunk][slot, away * count : (away + 1) * count, :] = turned[
                        pl.ds(start + first, count), :
                    ].astype(jnp.bfloat16)
                    first += count


def half_kernel(out_count, *refs):
    tile_ref = refs[0]
    parts = refs[1 : -1 - out_count]
    outs = refs[-1 - out_count : -1]
    wide = refs[-1]
    slot_count, block = tile_ref.shape[:2]
    width = parts[0].shape[1]
    rows = STEP_ROWS
    stride = rows + 1
    columns = []
    for slot in range(slot_count):
        total = parts[0][slot].astype(jnp.float32)
        for part in parts[1:]:
            total = total + part[slot].astype(jnp.float32)
        columns.append(total.astype(jnp.bfloat16))
    left = jnp.concatenate(columns, axis=1)

    def step(index, carry):
        base = pl.multiple_of(index * rows, rows)
        for row in range(0, rows, 2):
            right = jnp.concatenate(
                [
                    tile_ref[:, base + row + m].reshape(slot_count * block, block) for m in range(2)
                ],
                axis=1,
            )
            product = jnp.dot(left, right, preferred_element_type=jnp.float32)
            wide[pl.ds(row, width, stride=stride), :] = product[:, :block]
            wide[pl.ds(row + 1, width, stride=stride), :] = product[:, block:]
        first = 0
        for out in outs:
            for i in range(out.shape[0]):
                out[i, pl.ds(base, rows), :] = wide[pl.ds((first + i) * stride, rows), :].astype(
                    jnp.bfloat16
                )
            first += out.shape[0]
        return carry

    lax.fori_loop(0, block // rows, step, 0)


def gram(fitted, parts, first):
    count = len(fitted)
    right = [
        part[i if part is parts[-1] else first + i] for i in range(count) for part in parts
    ]
    return lax.dot_general(
        jnp.concatenate(fitted, axis=1),
        jnp.concatenate(right, axis=1),
        (((1,), (1,)), ((), ())),
        preferred_element_type=jnp.float32,
    )


def fit_kernel(aux_count, first, *refs):
    metric_ref = refs[0]
    parts = refs[1 : 1 + aux_count]
    before = refs[1 + aux_count : -2]
    fitted_ref, after_ref = refs[-2:]
    count, block, width = parts[-1].shape
    metric = metric_ref[...]
    for start in range(0, count, GROUP):
        here = min(GROUP, count - start)
        rows = [part[first + start : first + start + here] for part in parts[:-1]]
        rows.append(parts[-1][start : start + here])
        half = jnp.concatenate([x.reshape(here * block, width) for x in rows], axis=1)
        fitted = jnp.dot(half, metric, preferred_element_type=jnp.float32).astype(jnp.bfloat16)
        fitted_ref[start : start + here] = fitted.reshape(here, block, aux_count * width)
    total = gram([fitted_ref[i] for i in range(count)], parts, first)
    for ref in before:
        total = total + ref[...]
    after_ref[...] = total


def couple_kernel(aux_count, first, final, *refs):
    total = gram([refs[0][i] for i in range(refs[0].shape[0])], refs[1 : 1 + aux_count], first)
    before = refs[1 + aux_count : -1]
    if final:
        before, diagonal = before[:-1], before[-1]
    for ref in before:
        total = total + ref[...]
    if final:
        block = total.shape[0]
        refs[-1][:, :block] = diagonal[...].astype(jnp.bfloat16)
        refs[-1][:, block:] = total.astype(jnp.bfloat16)
    else:
        refs[-1][...] = total


def on_device(orb_count, aux_count, three_center, screening, density_factor, metric_inverse):
    slot_count, block = three_center.shape[:2]
    occupied = density_factor.shape[1]
    owned = density_factor.shape[0] // block
    share = occupied // aux_count
    chunk_rows = [share * part // sum(PARTS) for part in PARTS]
    chunks = len(chunk_rows)
    bf16, f32 = jnp.bfloat16, jnp.float32

    orb = lax.axis_index("orb")
    aux = lax.axis_index("aux")
    place = jnp.stack([(orb >> 1) * (2 * owned), orb & 1, aux]).astype(jnp.int32)

    def along_orb(x, by):
        return lax.ppermute(x, "orb", [(i, (i + by) % orb_count) for i in range(orb_count)])

    def same_core(x, chip):
        return lax.ppermute(x, "orb", [(i, i ^ (2 * chip)) for i in range(orb_count)])

    def across_aux(x, away):
        return lax.ppermute(x, "aux", [(i, i ^ away) for i in range(aux_count)])

    turned = local_call(
        functools.partial(turn_kernel, aux_count),
        jax.ShapeDtypeStruct(metric_inverse.shape, bf16),
        [metric_inverse],
        [place],
        LONG,
    )
    partner = lax.ppermute(density_factor, "orb", [(i, i ^ 1) for i in range(orb_count)])
    wanted = [screening]
    chips = range(1, orb_count // 2)
    for chip in chips:
        wanted.append(same_core(screening, chip))
    given = local_call(
        functools.partial(pick_kernel, owned, block, slot_count, aux_count, chunk_rows),
        [
            jax.ShapeDtypeStruct((slot_count, aux_count * count, block), bf16)
            for _ in wanted
            for count in chunk_rows
        ],
        [density_factor, partner],
        [place, *wanted],
        LONG,
        [pltpu.VMEM((occupied, block), f32)],
    )
    last = aux_count - 1
    pieces = []
    for c, count in enumerate(chunk_rows):
        arrived = [given[c]]
        for chip in chips:
            arrived.append(same_core(given[chip * chunks + c], chip))
        piece_rows = [count * part // sum(PIECES[c]) for part in PIECES[c]]
        out_rows = [count] * last + piece_rows
        halves = local_call(
            functools.partial(half_kernel, len(out_rows)),
            [jax.ShapeDtypeStruct((rows, block, block), bf16) for rows in out_rows],
            [three_center, *arrived],
            [],
            2 * slot_count * block**3 * count * aux_count,
            [pltpu.VMEM((aux_count * count * (STEP_ROWS + 1), block), f32)],
        )
        mine, theirs = [halves[0]], []
        for away in range(1, last):
            mine.append(across_aux(halves[away], away))
        for away in range(last):
            theirs.append(along_orb(mine[away], -1))
        for j, rows in enumerate(piece_rows):
            mine_piece = across_aux(halves[last + j], last)
            their_piece = along_orb(mine_piece, -1)
            pieces.append((c, j, sum(piece_rows[:j]), rows, mine + [mine_piece], theirs + [their_piece]))

    diagonal, coupling = [], []
    width = aux_count * block
    for number, (c, j, first, count, mine, theirs) in enumerate(pieces):
        final = number == len(pieces) - 1
        fitted, *diagonal = local_call(
            functools.partial(fit_kernel, aux_count, first),
            [
                jax.ShapeDtypeStruct((count, block, width), bf16),
                jax.ShapeDtypeStruct((block, block), f32),
            ],
            [turned, *mine, *diagonal],
            [],
            2 * count * block * width * (width + block),
        )
        coupling = [
            local_call(
                functools.partial(couple_kernel, aux_count, first, final),
                jax.ShapeDtypeStruct((block, 2 * block), bf16)
                if final
                else jax.ShapeDtypeStruct((block, block), f32),
                [fitted, *theirs, *coupling, *(diagonal if final else [])],
                [],
                2 * count * block * width * block,
            )
        ]

    terms = {0: coupling[0]}
    for away in reversed(range(1, aux_count)):
        terms[away] = across_aux(coupling[0], away)
    terms = [terms[away].astype(f32) for away in range(aux_count)]
    while len(terms) > 1:
        terms = [a + b for a, b in zip(terms[::2], terms[1::2])]
    return terms[0].astype(bf16)


def solution(mesh):
    placed = (P(("orb", "aux"), None, None, None), P(("orb", "aux"), None), P("orb", None), P())
    sizes = mesh.shape["orb"], mesh.shape["aux"]

    def body(*args):
        return on_device(*sizes, *args)

    return jax.shard_map(body, mesh=mesh, in_specs=placed, out_specs=P("orb", None), check_vma=False)
```

```python
import functools

import jax
import jax.numpy as jnp
from jax import lax
from jax.experimental import pallas as pl
from jax.experimental.pallas import tpu as pltpu
from jax.sharding import PartitionSpec as P


PARTS = (3, 5)
PIECES = ((1,), (2, 2, 1))
STEP_ROWS = 16
GROUP = 4
LONG = 20_000_000_000
VMEM = pltpu.VMEM
SMEM_SPEC = pl.BlockSpec(memory_space=pltpu.SMEM)
VMEM_SPEC = pl.BlockSpec(memory_space=pltpu.VMEM)


def local_call(kernel, out_shape, operands, scalars, flops, scratch=()):
    operands = [pltpu.with_memory_space_constraint(x, VMEM) for x in operands]
    out_shape = jax.tree.map(lambda x: VMEM(x.shape, x.dtype), out_shape)
    return pl.pallas_call(
        kernel,
        out_shape=out_shape,
        in_specs=[SMEM_SPEC] * len(scalars) + [VMEM_SPEC] * len(operands),
        out_specs=jax.tree.map(lambda _: VMEM_SPEC, out_shape),
        scratch_shapes=list(scratch),
        cost_estimate=pl.CostEstimate(flops=flops, bytes_accessed=1 << 20, transcendentals=0),
        compiler_params=pltpu.CompilerParams(vmem_limit_bytes=12 << 20),
    )(*scalars, *operands)


def turn_kernel(aux_count, place_ref, metric_ref, turned_ref):
    width = metric_ref.shape[0] // aux_count
    me = place_ref[2]
    for row in range(aux_count):
        for column in range(aux_count):
            turned_ref[row * width : (row + 1) * width, column * width : (column + 1) * width] = (
                metric_ref[
                    pl.ds(pl.multiple_of((me ^ row) * width, width), width),
                    pl.ds(pl.multiple_of((me ^ column) * width, width), width),
                ]
            )


def pick_kernel(owned, block, slot_count, aux_count, chunk_rows, *refs):
    dest_count = (len(refs) - 4) // (1 + len(chunk_rows))
    place_ref = refs[0]
    wanted = refs[1 : 1 + dest_count]
    own_ref, partner_ref = refs[1 + dest_count : 3 + dest_count]
    given = refs[3 + dest_count : -1]
    turned = refs[-1]
    base, core, me = place_ref[0], place_ref[1], place_ref[2]
    share = turned.shape[0] // aux_count
    for dest in range(dest_count):
        for slot in range(slot_count):
            orbital = wanted[dest][slot, 1]
            local = orbital - base
            inside = (orbital >= 0) & (local >= 0) & (local < 2 * owned)
            upper = jnp.where(local >= owned, 1, 0)
            row = jnp.clip(local - upper * owned, 0, owned - 1) * block
            rows = pl.ds(pl.multiple_of(row, block), block)
            picked = jnp.where(
                upper == core, own_ref[rows, :].astype(jnp.float32), partner_ref[rows, :].astype(jnp.float32)
            )
            picked = jnp.where(inside, picked, jnp.zeros_like(picked))
            turned[...] = picked.T
            for away in range(aux_count):
                start = pl.multiple_of((me ^ away) * share, share)
                first = 0
                for chunk, count in enumerate(chunk_rows):
                    given[dest * len(chunk_rows) + chunk][slot, away * count : (away + 1) * count, :] = turned[
                        pl.ds(start + first, count), :
                    ].astype(jnp.bfloat16)
                    first += count


def half_kernel(out_count, *refs):
    tile_ref = refs[0]
    parts = refs[1 : -1 - out_count]
    outs = refs[-1 - out_count : -1]
    wide = refs[-1]
    slot_count, block = tile_ref.shape[:2]
    width = parts[0].shape[1]
    rows = STEP_ROWS
    stride = rows + 1
    columns = []
    for slot in range(slot_count):
        total = parts[0][slot].astype(jnp.float32)
        for part in parts[1:]:
            total = total + part[slot].astype(jnp.float32)
        columns.append(total.astype(jnp.bfloat16))
    left = jnp.concatenate(columns, axis=1)

    def step(index, carry):
        base = pl.multiple_of(index * rows, rows)
        for row in range(0, rows, 2):
            right = jnp.concatenate(
                [
                    tile_ref[:, base + row + m].reshape(slot_count * block, block) for m in range(2)
                ],
                axis=1,
            )
            product = jnp.dot(left, right, preferred_element_type=jnp.float32)
            wide[pl.ds(row, width, stride=stride), :] = product[:, :block]
            wide[pl.ds(row + 1, width, stride=stride), :] = product[:, block:]
        first = 0
        for out in outs:
            for i in range(out.shape[0]):
                out[i, pl.ds(base, rows), :] = wide[pl.ds((first + i) * stride, rows), :].astype(
                    jnp.bfloat16
                )
            first += out.shape[0]
        return carry

    lax.fori_loop(0, block // rows, step, 0)


def gram(fitted, parts, first):
    count = len(fitted)
    right = [
        part[i if part is parts[-1] else first + i] for i in range(count) for part in parts
    ]
    return lax.dot_general(
        jnp.concatenate(fitted, axis=1),
        jnp.concatenate(right, axis=1),
        (((1,), (1,)), ((), ())),
        preferred_element_type=jnp.float32,
    )


def fit_kernel(aux_count, first, *refs):
    metric_ref = refs[0]
    parts = refs[1 : 1 + aux_count]
    before = refs[1 + aux_count : -2]
    fitted_ref, after_ref = refs[-2:]
    count, block, width = parts[-1].shape
    metric = metric_ref[...]
    for start in range(0, count, GROUP):
        here = min(GROUP, count - start)
        rows = [part[first + start : first + start + here] for part in parts[:-1]]
        rows.append(parts[-1][start : start + here])
        half = jnp.concatenate([x.reshape(here * block, width) for x in rows], axis=1)
        fitted = jnp.dot(half, metric, preferred_element_type=jnp.float32).astype(jnp.bfloat16)
        fitted_ref[start : start + here] = fitted.reshape(here, block, aux_count * width)
    total = gram([fitted_ref[i] for i in range(count)], parts, first)
    for ref in before:
        total = total + ref[...]
    after_ref[...] = total


def couple_kernel(aux_count, first, final, *refs):
    parts, before = refs[1 : 1 + aux_count], refs[1 + aux_count : -1]
    total = gram([refs[0][i] for i in range(refs[0].shape[0])], parts, first)
    if final:
        before, diagonal = before[:-1], before[-1]
    for ref in before:
        total = total + ref[...]
    if final:
        block = total.shape[0]
        refs[-1][:, :block] = diagonal[...].astype(refs[-1].dtype)
        refs[-1][:, block:] = total.astype(refs[-1].dtype)
    else:
        refs[-1][...] = total


def on_device(orb_count, aux_count, three_center, screening, density_factor, metric_inverse):
    slot_count, block = three_center.shape[:2]
    occupied = density_factor.shape[1]
    owned = density_factor.shape[0] // block
    share = occupied // aux_count
    chunk_rows = [share * part // sum(PARTS) for part in PARTS]
    chunks = len(chunk_rows)
    bf16, f32 = jnp.bfloat16, jnp.float32

    orb = lax.axis_index("orb")
    aux = lax.axis_index("aux")
    place = jnp.stack([(orb >> 1) * (2 * owned), orb & 1, aux]).astype(jnp.int32)

    def to_previous(x):
        return lax.ppermute(x, "orb", [(i, (i - 1) % orb_count) for i in range(orb_count)])

    def same_core(x, chip):
        return lax.ppermute(x, "orb", [(i, i ^ (2 * chip)) for i in range(orb_count)])

    def across_aux(x, away):
        return lax.ppermute(x, "aux", [(i, i ^ away) for i in range(aux_count)])

    turned = local_call(
        functools.partial(turn_kernel, aux_count),
        jax.ShapeDtypeStruct(metric_inverse.shape, bf16),
        [metric_inverse],
        [place],
        LONG,
    )
    partner = lax.ppermute(density_factor, "orb", [(i, i ^ 1) for i in range(orb_count)])
    wanted = [screening]
    chips = range(1, orb_count // 2)
    for chip in chips:
        wanted.append(same_core(screening, chip))
    given = local_call(
        functools.partial(pick_kernel, owned, block, slot_count, aux_count, chunk_rows),
        [
            jax.ShapeDtypeStruct((slot_count, aux_count * count, block), bf16)
            for _ in wanted
            for count in chunk_rows
        ],
        [density_factor, partner],
        [place, *wanted],
        LONG,
        [pltpu.VMEM((occupied, block), f32)],
    )
    last = aux_count - 1
    pieces = []
    for c, count in enumerate(chunk_rows):
        arrived = [given[c]]
        for chip in chips:
            arrived.append(same_core(given[chip * chunks + c], chip))
        piece_rows = [count * part // sum(PIECES[c]) for part in PIECES[c]]
        out_rows = [count] * last + piece_rows
        halves = local_call(
            functools.partial(half_kernel, len(out_rows)),
            [jax.ShapeDtypeStruct((rows, block, block), bf16) for rows in out_rows],
            [three_center, *arrived],
            [],
            2 * slot_count * block**3 * count * aux_count,
            [pltpu.VMEM((aux_count * count * (STEP_ROWS + 1), block), f32)],
        )
        mine, theirs = [halves[0]], []
        for away in range(1, last):
            mine.append(across_aux(halves[away], away))
        for away in range(last):
            theirs.append(to_previous(mine[away]))
        for j, rows in enumerate(piece_rows):
            mine_piece = across_aux(halves[last + j], last)
            their_piece = to_previous(mine_piece)
            pieces.append((c, j, sum(piece_rows[:j]), rows, mine + [mine_piece], theirs + [their_piece]))

    diagonal, coupling = [], []
    width = aux_count * block
    for number, (c, j, first, count, mine, theirs) in enumerate(pieces):
        final = number == len(pieces) - 1
        fitted, *diagonal = local_call(
            functools.partial(fit_kernel, aux_count, first),
            [
                jax.ShapeDtypeStruct((count, block, width), bf16),
                jax.ShapeDtypeStruct((block, block), f32),
            ],
            [turned, *mine, *diagonal],
            [],
            2 * count * block * width * (width + block),
        )
        coupling = [
            local_call(
                functools.partial(couple_kernel, aux_count, first, final),
                jax.ShapeDtypeStruct((block, 2 * block), bf16)
                if final
                else jax.ShapeDtypeStruct((block, block), f32),
                [fitted, *theirs, *coupling, *(diagonal if final else [])],
                [],
                2 * count * block * width * block,
            )
        ]

    terms = {0: coupling[0]}
    for away in reversed(range(1, aux_count)):
        terms[away] = across_aux(coupling[0], away)
    terms = [terms[away].astype(f32) for away in range(aux_count)]
    while len(terms) > 1:
        terms = [a + b for a, b in zip(terms[::2], terms[1::2])]
    return terms[0].astype(bf16)


def solution(mesh):
    placed = (P(("orb", "aux"), None, None, None), P(("orb", "aux"), None), P("orb", None), P())
    sizes = mesh.shape["orb"], mesh.shape["aux"]

    def body(*args):
        return on_device(*sizes, *args)

    return jax.shard_map(body, mesh=mesh, in_specs=placed, out_specs=P("orb", None), check_vma=False)
```
